32 devices in a mesh: gossip: 16 (over z, x, core), tensor: 2 (over y).
Axes of the slice: x: 2, y: 2, z: 4, core: 2. Of those that a mesh axis runs over, the one named last changes fastest.
Arguments:
- weights: float32 [16, 8192, 1024], P('gossip', 'tensor'), may hold values from -6 to 6
- updates: bfloat16 [16, 2, 8192, 1024], P('gossip', None, 'tensor'), may hold values from -4 to 4
- factors: bfloat16 [3, 1024, 128], replicated, may hold values from -6 to 6
- partners: int32 [3, 16], replicated, may hold values from 0 to 15, as said below
Outputs:
- averaged: float32 [16, 8192, 1024], P('gossip', 'tensor')
The draws below stay inside these ranges and needn't reach their ends.
Inputs may be any that keep to these rules, and one draw needn't show every extreme that they name: Row k pairs replica i with replica i XOR c_k, for one offset c_k of 1 to 15 a row; so each row is a perfect matching and partners[k, partners[k, i]] = i.
All inputs are finite; a program needn't handle non-finite values.
Results may differ from the reference program's by a relative error of at most 0.0003.
Values sent between devices are 32-bit elements; how exact they have to be, the bound alone decides.
No kernel may reach another device: no remote copies, remote signals or barrier semaphores. Data moves between devices by JAX's collectives and lax.ppermute only.
A program may use at most 128 MiB of HBM per device.

```python
import jax
import jax.numpy as jnp
from jax import lax

D = 8192
KV = 1024
RANK = 128
MATCHINGS = 3
REPLICAS = 16
N_GOSSIP = 16


def draw_partners(key, part):
    offsets = jax.random.randint(jax.random.fold_in(key, 17), (MATCHINGS, 1), 1, N_GOSSIP)
    indices = jnp.arange(N_GOSSIP, dtype=jnp.int32)[None, :]
    return jnp.bitwise_xor(indices, offsets.astype(jnp.int32)).astype(jnp.int32)


def block_levels(rng, dims, shards, smallest, largest):
    level, own = 1.0, jax.random.fold_in(rng, 6)
    for position, parts in shards:
        steps = jnp.exp(jax.random.uniform(jax.random.fold_in(own, position), (parts,), jnp.float32, smallest / len(shards), largest / len(shards)))
        level = level * jnp.repeat(steps, dims[position] // parts).reshape([-1 if axis == position else 1 for axis in range(len(dims))])
    return level


def normal_values(rng, extent, scale, reach, cuts=(), kind=jnp.bfloat16):
    entries = jax.random.normal(rng, extent, jnp.float32) * scale
    if len(cuts) > 0:
        entries = block_levels(rng, extent, cuts, -0.22, 0.18) * entries
    return jnp.clip(entries, min=-reach, max=reach).astype(kind)


def setup_inputs(seed: int = 0) -> dict:
    streams_of = jax.random.split(jax.random.key(seed), 5)
    return {
        "weights": normal_values(streams_of[0], (REPLICAS, D, KV), 1.0, 6.0, ((0, 16), (1, 2)), jnp.float32),
        "updates": normal_values(streams_of[1], (REPLICAS, MATCHINGS - 1, D, KV), 0.5, 4.0, ((0, 16), (2, 2))),
        "factors": normal_values(streams_of[2], (MATCHINGS, KV, RANK), 1.0, 6.0),
        "partners": draw_partners(jax.random.fold_in(streams_of[4], 71), 0),
    }


def orthonormal(factor_low, left_block):
    return jax.scipy.linalg.solve_triangular(factor_low, left_block.T, lower=True).T

def reference(weights, updates, factors, partners):
    highest = lax.Precision.HIGHEST
    replicas = weights
    for matching in range(MATCHINGS):
        if matching > 0:
            replicas = replicas - updates[:, matching - 1].astype(jnp.float32)
        right_start = factors[matching].astype(jnp.float32)
        partner_ids = partners[matching].astype(jnp.int32)
        own_left = jnp.einsum('rdk,kq->rdq', replicas, right_start, precision=highest)
        left_block = own_left - own_left[partner_ids]
        gram_total = jnp.einsum('rdq,rdp->rqp', left_block, left_block, precision=highest)
        factor_low = jax.vmap(jnp.linalg.cholesky)(gram_total)
        ortho = jax.vmap(orthonormal)(factor_low, left_block)
        partial_value = jnp.einsum('rdk,rdq->rkq', replicas, ortho, precision=highest)
        right_total = partial_value + partial_value[partner_ids]
        replicas = replicas - 0.5 * jnp.einsum('rdq,rkq->rdk', ortho, right_total, precision=highest)
    return replicas
```

```python
import functools

import jax
import jax.numpy as jnp
from jax import lax
from jax.experimental import pallas as pl
from jax.experimental.pallas import tpu as pltpu
from jax.sharding import PartitionSpec as P

MATCHINGS = 3
RANK = 128
BLOCK = 8
SPLIT_ROWS = 16
F32 = jnp.float32
BF16 = jnp.bfloat16


def split(value):
    high = value.astype(BF16)
    low = (value - high.astype(F32)).astype(BF16)
    return high, low


def dot(first, second):
    return jnp.dot(first, second, preferred_element_type=F32)


def dot_exact(first, second):
    return jnp.dot(first, second, precision=lax.Precision.HIGHEST, preferred_element_type=F32)


def params(mib=48):
    return pltpu.CompilerParams(vmem_limit_bytes=mib * 1024 * 1024)


def product_kernel(w_ref, q_ref, y_ref):
    high, low = split(w_ref[...])
    y_ref[...] = dot(high, q_ref[...]) + dot(low, q_ref[...])


def first_product(weights, factors):
    _, rows, width = weights.shape
    tile = rows // 8
    return pl.pallas_call(
        product_kernel,
        grid=(rows // tile,),
        in_specs=[
            pl.BlockSpec((None, tile, width), lambda i: (0, i, 0)),
            pl.BlockSpec((None, width, RANK), lambda i: (0, 0, 0)),
        ],
        out_specs=pl.BlockSpec((tile, RANK), lambda i: (i, 0)),
        out_shape=jax.ShapeDtypeStruct((rows, RANK), F32),
        compiler_params=params(),
        cost_estimate=pl.CostEstimate(
            flops=4 * rows * width * RANK, bytes_accessed=4 * rows * width, transcendentals=0
        ),
        name="first_product",
    )(weights, factors)


def each_column(width, body):
    block = min(2 * RANK, width)

    def step(index, carry):
        body(index == 0, pl.ds(pl.multiple_of(index * block, block), block))
        return carry

    lax.fori_loop(0, width // block, step, 0)


def stacked_update(left, base, stack_ref, low_ref):
    high, low = split(left)
    return base + dot(jnp.concatenate([high, low], axis=1), stack_ref[...]) + dot(high, low_ref[...])


def fill_stack(inverse_ref, right_ref, stack_ref, low_ref):
    def column(_, columns):
        high, low = split(-0.5 * dot_exact(inverse_ref[...], right_ref[:, columns]))
        stack_ref[:RANK, columns] = high
        stack_ref[RANK:, columns] = high
        low_ref[:, columns] = low

    each_column(right_ref.shape[1], column)


def left_specs(rows, tile):
    early = rows // 4 * 3 // tile
    return early, [
        pl.BlockSpec((tile, RANK), lambda i: (jnp.minimum(i, early - 1), 0)),
        pl.BlockSpec((tile, RANK), lambda i: (jnp.maximum(i - early, 0), 0)),
    ]


def left_rows(early, early_ref, late_ref):
    return jnp.where(pl.program_id(0) < early, early_ref[...], late_ref[...])


def advance_kernel(early, updating, looking, *refs):
    refs = list(refs)
    w_ref = refs.pop(0)
    if updating:
        before_ref, early_ref, late_ref, inverse_ref, right_ref = refs[:5]
        refs = refs[5:]
    if looking:
        after_ref, q_ref = refs[:2]
        refs = refs[2:]
    if updating:
        new_ref = refs.pop(0)
    if looking:
        z_ref, v_ref = refs[:2]
        refs = refs[2:]
    now = w_ref[...]
    if updating:
        stack_ref, low_ref = refs

        @pl.when(pl.program_id(0) == 0)
        def _():
            fill_stack(inverse_ref, right_ref, stack_ref, low_ref)

        left = left_rows(early, early_ref, late_ref)
        now = stacked_update(left, now - before_ref[...].astype(F32), stack_ref, low_ref)
        new_ref[...] = now
    if looking:
        high, low = split(now)
        z = dot(high, q_ref[...]) + dot(low, q_ref[...])
        z_ref[...] = z
        v_ref[...] = z - dot(after_ref[...], q_ref[...])


def advance(matching, replica, updates, factors, previous):
    rows, width = updates.shape[2:]
    tile = rows // SPLIT_ROWS
    updating, looking = matching > 0, matching < MATCHINGS - 1
    w_spec = pl.BlockSpec((None, tile, width), lambda i: (0, i, 0))
    row_spec = pl.BlockSpec((tile, RANK), lambda i: (i, 0))
    early, pair_specs = left_specs(rows, tile)
    operands, specs, outs, out_specs, scratch = [replica], [w_spec], [], [], []
    if updating:
        left, inverse, right = previous
        operands += [updates, *left, inverse, right]
        specs += [
            pl.BlockSpec((None, None, tile, width), lambda i: (0, matching - 1, i, 0)),
            *pair_specs,
            pl.BlockSpec((RANK, RANK), lambda i: (0, 0)),
            pl.BlockSpec((RANK, width), lambda i: (0, 0)),
        ]
        outs.append(jax.ShapeDtypeStruct((1, rows, width), F32))
        out_specs.append(w_spec)
        scratch = [pltpu.VMEM((2 * RANK, width), BF16), pltpu.VMEM((RANK, width), BF16)]
    if looking:
        operands += [updates, factors]
        specs += [
            pl.BlockSpec((None, None, tile, width), lambda i: (0, matching, i, 0)),
            pl.BlockSpec((None, width, RANK), lambda i: (matching + 1, 0, 0)),
        ]
        outs += [jax.ShapeDtypeStruct((rows, RANK), F32)] * 2
        out_specs += [row_spec] * 2
    return pl.pallas_call(
        functools.partial(advance_kernel, early, updating, looking),
        grid=(rows // tile,),
        in_specs=specs,
        out_specs=out_specs,
        out_shape=outs,
        scratch_shapes=scratch,
        compiler_params=params(),
        cost_estimate=pl.CostEstimate(
            flops=10 * rows * width * RANK, bytes_accessed=12 * rows * width, transcendentals=0
        ),
        name=f"advance_{matching}",
    )(*operands)


def gather_kernel(looking, chained, *refs):
    refs = list(refs)
    y_ref, b_ref, w_ref = refs[:3]
    refs = refs[3:]
    if looking:
        z_ref = refs.pop(0)
    if chained:
        in_small_ref, in_large_ref = refs[:2]
        refs = refs[2:]
    left_ref, small_ref, large_ref, acc_small, acc_large = refs
    step = pl.program_id(0)

    left = y_ref[...] - b_ref[...]
    left_ref[...] = left
    turned = jnp.concatenate(split(left.T), axis=0)
    narrow = jnp.concatenate([left, z_ref[...]], axis=1) if looking else left
    high, low = split(narrow)
    first = step == 0
    acc_small[...] = jnp.where(first, 0.0, acc_small[...]) + (dot(turned, high) + dot(turned, low))
    high, low = split(w_ref[...])
    acc_large[...] = jnp.where(first, 0.0, acc_large[...]) + (dot(turned, high) + dot(turned, low))

    @pl.when(step == pl.num_programs(0) - 1)
    def _():
        small = acc_small[:RANK] + acc_small[RANK:]
        small_ref[...] = small + in_small_ref[...] if chained else small

        def column(_, columns):
            large = acc_large[:RANK, columns] + acc_large[RANK:, columns]
            large_ref[:, columns] = large + in_large_ref[:, columns] if chained else large

        each_column(large_ref.shape[1], column)


def gather(start, stop, own, other, replica, z, chain):
    rows, width = replica.shape[1:]
    tile = rows // SPLIT_ROWS
    base, steps = start // tile, (stop - start) // tile
    looking, chained = z is not None, chain is not None
    n_small = 2 * RANK if looking else RANK
    row_spec = pl.BlockSpec((tile, RANK), lambda i: (base + i, 0))
    small_spec = pl.BlockSpec((RANK, n_small), lambda i: (0, 0))
    large_spec = pl.BlockSpec((RANK, width), lambda i: (0, 0))
    operands = [own, other, replica]
    specs = [
        row_spec,
        pl.BlockSpec((tile, RANK), lambda i: (i, 0)),
        pl.BlockSpec((None, tile, width), lambda i: (0, base + i, 0)),
    ]
    if looking:
        operands.append(z)
        specs.append(row_spec)
    if chained:
        operands += chain
        specs += [small_spec, large_spec]
    return pl.pallas_call(
        functools.partial(gather_kernel, looking, chained),
        grid=(steps,),
        in_specs=specs,
        out_specs=[pl.BlockSpec((tile, RANK), lambda i: (i, 0)), small_spec, large_spec],
        out_shape=[
            jax.ShapeDtypeStruct((stop - start, RANK), F32),
            jax.ShapeDtypeStruct((RANK, n_small), F32),
            jax.ShapeDtypeStruct((RANK, width), F32),
        ],
        scratch_shapes=[pltpu.VMEM((2 * RANK, n_small), F32), pltpu.VMEM((2 * RANK, width), F32)],
        compiler_params=params(),
        cost_estimate=pl.CostEstimate(
            flops=8 * (stop - start) * width * RANK,
            bytes_accessed=4 * (stop - start) * width,
            transcendentals=0,
        ),
        name="gather_left",
    )(*operands)


def inverse_kernel(g_ref, mine_ref, work_ref):
    work_ref[...] = g_ref[...] + mine_ref[...]
    lane = lax.broadcasted_iota(jnp.int32, (BLOCK, RANK), 1)
    row = lax.broadcasted_iota(jnp.int32, (BLOCK, RANK), 0)
    wide = lax.broadcasted_iota(jnp.int32, (RANK, RANK), 1)

    def step(block, carry):
        first = pl.multiple_of(block * BLOCK, BLOCK)
        panel = work_ref[pl.ds(first, BLOCK), :]
        turned = pltpu.roll(panel, RANK - first, 1)
        columns = [jnp.broadcast_to(turned[:, c : c + 1], (BLOCK, RANK)) for c in range(BLOCK)]
        for j in range(BLOCK):
            pivot = 1.0 / jnp.broadcast_to(columns[j][j : j + 1], (BLOCK, RANK))
            for c in range(BLOCK):
                if c != j:
                    scaled = jnp.broadcast_to(columns[c][j : j + 1], (BLOCK, RANK)) * pivot
                    columns[c] = jnp.where(row == j, scaled, columns[c] - columns[j] * scaled)
            columns[j] = jnp.where(row == j, pivot, -columns[j] * pivot)
        across = jnp.zeros((BLOCK, RANK), F32)
        for c in range(BLOCK):
            across += columns[c] * jnp.broadcast_to(panel[c : c + 1], (BLOCK, RANK))
        for c in range(BLOCK):
            across = jnp.where(lane == first + c, columns[c], across)
        signed = jnp.where(lane < first, -panel, panel)
        change = lax.dot_general(
            signed,
            across,
            (((0,), (0,)), ((), ())),
            precision=lax.Precision.HIGHEST,
            preferred_element_type=F32,
        )
        inside = (wide >= first) & (wide < first + BLOCK)
        work_ref[...] = jnp.where(inside, 0.0, work_ref[...]) - change
        work_ref[pl.ds(first, BLOCK), :] = across
        return carry

    lax.fori_loop(0, RANK // BLOCK, step, 0)


def inverse_of(gram, other):
    square = pl.BlockSpec((RANK, RANK), lambda i: (0, 0))
    return pl.pallas_call(
        inverse_kernel,
        grid=(1,),
        in_specs=[square, square],
        out_specs=square,
        out_shape=jax.ShapeDtypeStruct((RANK, RANK), F32),
        compiler_params=params(),
        cost_estimate=pl.CostEstimate(flops=2 * 10**9, bytes_accessed=10**5, transcendentals=0),
        name="inverse",
    )(gram, other)


def correct_kernel(early, v_ref, early_ref, late_ref, inverse_ref, cross_ref, y_ref, *scratch):
    stack_ref, low_ref = scratch

    @pl.when(pl.program_id(0) == 0)
    def _():
        fill_stack(inverse_ref, cross_ref, stack_ref, low_ref)

    left = left_rows(early, early_ref, late_ref)
    y_ref[...] = stacked_update(left, v_ref[...], stack_ref, low_ref)


def correct(v, left, inverse, cross):
    rows = v.shape[0]
    tile = rows // 4
    row_spec = pl.BlockSpec((tile, RANK), lambda i: (i, 0))
    early, pair_specs = left_specs(rows, tile)
    square = pl.BlockSpec((RANK, RANK), lambda i: (0, 0))
    return pl.pallas_call(
        functools.partial(correct_kernel, early),
        grid=(rows // tile,),
        in_specs=[row_spec, *pair_specs, square, square],
        out_specs=row_spec,
        out_shape=jax.ShapeDtypeStruct((rows, RANK), F32),
        scratch_shapes=[pltpu.VMEM((2 * RANK, RANK), BF16), pltpu.VMEM((RANK, RANK), BF16)],
        compiler_params=params(),
        cost_estimate=pl.CostEstimate(
            flops=2 * 10**9, bytes_accessed=12 * rows * RANK, transcendentals=0
        ),
        name="correct",
    )(v, *left, inverse, cross)


def finish_kernel(early, w_ref, early_ref, late_ref, inverse_ref, right_ref, out_ref, *scratch):
    stack_ref, low_ref = scratch

    @pl.when(pl.program_id(0) == 0)
    def _():
        fill_stack(inverse_ref, right_ref, stack_ref, low_ref)

    left = left_rows(early, early_ref, late_ref)
    out_ref[...] = stacked_update(left, w_ref[...], stack_ref, low_ref)


def finish(replica, left, inverse, right):
    rows, width = replica.shape[1:]
    tile = rows // 8
    w_spec = pl.BlockSpec((None, tile, width), lambda i: (0, i, 0))
    early, pair_specs = left_specs(rows, tile)
    return pl.pallas_call(
        functools.partial(finish_kernel, early),
        grid=(rows // tile,),
        in_specs=[
            w_spec,
            *pair_specs,
            pl.BlockSpec((RANK, RANK), lambda i: (0, 0)),
            pl.BlockSpec((RANK, width), lambda i: (0, 0)),
        ],
        out_specs=w_spec,
        out_shape=jax.ShapeDtypeStruct(replica.shape, F32),
        scratch_shapes=[pltpu.VMEM((2 * RANK, width), BF16), pltpu.VMEM((RANK, width), BF16)],
        compiler_params=params(),
        name="finish",
    )(replica, *left, inverse, right)


def swap(value, offset):
    if offset == 0:
        return value
    return lax.ppermute(value, "gossip", [(i, i ^ offset) for i in range(lax.axis_size("gossip"))])


def keep(value):
    return value


def route(value, offset):
    for level in range(lax.axis_size("gossip").bit_length() - 1):
        moved = functools.partial(swap, offset=1 << level)
        value = lax.cond(offset >> level & 1 == 1, moved, keep, value)
    return value


def across(value):
    return lax.ppermute(value, "tensor", [(0, 1), (1, 0)])


def chips_step(matching, offset, replica, updates, factors, own, sent, previous):
    rows = replica.shape[1]
    cut = rows // 4 * 3
    early = swap(sent[:cut], offset)
    late = swap(sent[cut:], offset)
    if matching > 0:
        left, inverse, right = previous
        previous = left, inverse, right + across(right)
    outs = list(advance(matching, replica, updates, factors, previous))
    now = outs[0] if matching > 0 else replica
    z = outs[-2] if matching < MATCHINGS - 1 else None
    return outs, late, list(gather(0, cut, own, early, now, z, None))


def small_step(offset, left, small, large, v):
    large_other = swap(large, offset)
    other = across(small)
    inverse = inverse_of(small, other)
    cross = small[:, RANK:] + other[:, RANK:]
    own = correct(v, left, inverse, cross + swap(cross, offset))
    return inverse, own, large + large_other


def last_step(offset, small, large):
    half = RANK // 2
    one, two = large[:half], large[half:]
    two = two + swap(two, offset)
    one = one + across(one)
    other = across(small)
    inverse = inverse_of(small, other)
    one = one + swap(one, offset)
    two = two + across(two)
    return inverse, jnp.concatenate([one, two], axis=0)


def overlapped(weights, updates, factors, offsets):
    size = lax.axis_size("gossip")
    rows = weights.shape[1]
    cut = rows // 4 * 3
    replica, previous = weights, ()
    own = first_product(weights, factors)
    for matching in range(MATCHINGS):
        offset = offsets[matching]
        sent = lax.cond(offset & 1 == 1, functools.partial(swap, offset=1), keep, own)
        branches = [
            functools.partial(chips_step, matching, choice) for choice in range(0, size, 2)
        ]
        outs, late, chain = lax.switch(
            offset >> 1, branches, replica, updates, factors, own, sent, previous
        )
        if matching > 0:
            replica, *outs = outs
        z, v = outs if outs else (None, None)
        early_left, *chain = chain
        late_left, small, large = gather(cut, rows, own, late, replica, z, chain)
        left = early_left, late_left
        step, operands = last_step, (small, large)
        if z is not None:
            step, operands = small_step, (left, small, large, v)
        branches = [functools.partial(step, choice) for choice in range(1, size)]
        state = lax.switch(offset - 1, branches, *operands)
        if z is not None:
            inverse, own, right = state
            previous = left, inverse, right
    inverse, right = state
    return finish(replica, left, inverse, right)


def plain(weights, updates, factors, offsets):
    rows = weights.shape[1]
    cut = rows // 4 * 3
    replica, previous = weights, ()
    own = first_product(weights, factors)
    for matching in range(MATCHINGS):
        offset = offsets[matching]
        other = route(own, offset)
        outs = list(advance(matching, replica, updates, factors, previous))
        if matching > 0:
            replica, *outs = outs
        z, v = outs if outs else (None, None)
        early_left, *chain = gather(0, cut, own, other[:cut], replica, z, None)
        late_left, small, large = gather(cut, rows, own, other[cut:], replica, z, chain)
        left = early_left, late_left
        both = lax.psum(jnp.concatenate([small, large], axis=1), "tensor")
        gram, both = both[:, :RANK], both[:, RANK:]
        both = both + route(both, offset)
        inverse = inverse_of(gram, jnp.zeros_like(gram))
        if z is not None:
            own = correct(v, left, inverse, both[:, :RANK])
            both = both[:, RANK:]
        previous = left, inverse, both
    return finish(replica, *previous)


def per_device(weights, updates, factors, partners):
    myself = lax.axis_index("gossip")
    mine = lax.dynamic_index_in_dim(partners, myself, axis=1, keepdims=False)
    offsets = [jnp.bitwise_xor(mine[matching], myself) for matching in range(MATCHINGS)]
    small_slice = lax.axis_size("tensor") == 2 and lax.axis_size("gossip") <= 16
    body = overlapped if small_slice else plain
    return body(weights, updates, factors, offsets)


def solution(mesh):
    placed = (P("gossip", "tensor", None), P("gossip", None, "tensor", None), P(), P())
    return jax.shard_map(
        per_device,
        mesh=mesh,
        in_specs=placed,
        out_specs=P("gossip", "tensor", None),
        check_vma=False,
    )
```

```python
import functools

import jax
import jax.numpy as jnp
from jax import lax
from jax.experimental import pallas as pl
from jax.experimental.pallas import tpu as pltpu
from jax.sharding import PartitionSpec as P

MATCHINGS = 3
RANK = 128
BLOCK = 8
SPLIT_ROWS = 16
F32 = jnp.float32
BF16 = jnp.bfloat16


def split(value):
    high = value.astype(BF16)
    low = (value - high.astype(F32)).astype(BF16)
    return high, low


def dot(first, second):
    return jnp.dot(first, second, preferred_element_type=F32)


def dot_exact(first, second):
    return jnp.dot(first, second, precision=lax.Precision.HIGHEST, preferred_element_type=F32)


def params(mib=48):
    return pltpu.CompilerParams(vmem_limit_bytes=mib * 1024 * 1024)


def product_kernel(w_ref, q_ref, y_ref):
    high, low = split(w_ref[...])
    y_ref[...] = dot(high, q_ref[...]) + dot(low, q_ref[...])


def first_product(weights, factors):
    _, rows, width = weights.shape
    tile = rows // 8
    return pl.pallas_call(
        product_kernel,
        grid=(rows // tile,),
        in_specs=[
            pl.BlockSpec((None, tile, width), lambda i: (0, i, 0)),
            pl.BlockSpec((None, width, RANK), lambda i: (0, 0, 0)),
        ],
        out_specs=pl.BlockSpec((tile, RANK), lambda i: (i, 0)),
        out_shape=jax.ShapeDtypeStruct((rows, RANK), F32),
        compiler_params=params(),
        cost_estimate=pl.CostEstimate(
            flops=4 * rows * width * RANK, bytes_accessed=4 * rows * width, transcendentals=0
        ),
        name="first_product",
    )(weights, factors)


def each_column(width, body):
    block = min(2 * RANK, width)

    def step(index, carry):
        body(index == 0, pl.ds(pl.multiple_of(index * block, block), block))
        return carry

    lax.fori_loop(0, width // block, step, 0)


def stacked_update(left, base, stack_ref, low_ref):
    high, low = split(left)
    return base + dot(jnp.concatenate([high, low], axis=1), stack_ref[...]) + dot(high, low_ref[...])


def fill_stack(inverse_ref, right_ref, stack_ref, low_ref):
    def column(_, columns):
        high, low = split(-0.5 * dot_exact(inverse_ref[...], right_ref[:, columns]))
        stack_ref[:RANK, columns] = high
        stack_ref[RANK:, columns] = high
        low_ref[:, columns] = low

    each_column(right_ref.shape[1], column)


def left_specs(rows, tile):
    early = rows // 4 * 3 // tile
    return early, [
        pl.BlockSpec((tile, RANK), lambda i: (jnp.minimum(i, early - 1), 0)),
        pl.BlockSpec((tile, RANK), lambda i: (jnp.maximum(i - early, 0), 0)),
    ]


def left_rows(early, early_ref, late_ref):
    return jnp.where(pl.program_id(0) < early, early_ref[...], late_ref[...])


def advance_kernel(early, updating, looking, *refs):
    refs = list(refs)
    w_ref = refs.pop(0)
    if updating:
        before_ref, early_ref, late_ref, inverse_ref, right_ref = refs[:5]
        refs = refs[5:]
    if looking:
        after_ref, q_ref = refs[:2]
        refs = refs[2:]
    if updating:
        new_ref = refs.pop(0)
    if looking:
        z_ref, v_ref = refs[:2]
        refs = refs[2:]
    now = w_ref[...]
    if updating:
        stack_ref, low_ref = refs

        @pl.when(pl.program_id(0) == 0)
        def _():
            fill_stack(inverse_ref, right_ref, stack_ref, low_ref)

        left = left_rows(early, early_ref, late_ref)
        now = stacked_update(left, now - before_ref[...].astype(F32), stack_ref, low_ref)
        new_ref[...] = now
    if looking:
        high, low = split(now)
        z = dot(high, q_ref[...]) + dot(low, q_ref[...])
        z_ref[...] = z
        v_ref[...] = z - dot(after_ref[...], q_ref[...])


def advance(matching, replica, updates, factors, previous):
    rows, width = updates.shape[2:]
    tile = rows // SPLIT_ROWS
    updating, looking = matching > 0, matching < MATCHINGS - 1
    w_spec = pl.BlockSpec((None, tile, width), lambda i: (0, i, 0))
    row_spec = pl.BlockSpec((tile, RANK), lambda i: (i, 0))
    early, pair_specs = left_specs(rows, tile)
    operands, specs, outs, out_specs, scratch = [replica], [w_spec], [], [], []
    if updating:
        left, inverse, right = previous
        operands += [updates, *left, inverse, right]
        specs += [
            pl.BlockSpec((None, None, tile, width), lambda i: (0, matching - 1, i, 0)),
            *pair_specs,
            pl.BlockSpec((RANK, RANK), lambda i: (0, 0)),
            pl.BlockSpec((RANK, width), lambda i: (0, 0)),
        ]
        outs.append(jax.ShapeDtypeStruct((1, rows, width), F32))
        out_specs.append(w_spec)
        scratch = [pltpu.VMEM((2 * RANK, width), BF16), pltpu.VMEM((RANK, width), BF16)]
    if looking:
        operands += [updates, factors]
        specs += [
            pl.BlockSpec((None, None, tile, width), lambda i: (0, matching, i, 0)),
            pl.BlockSpec((None, width, RANK), lambda i: (matching + 1, 0, 0)),
        ]
        outs += [jax.ShapeDtypeStruct((rows, RANK), F32)] * 2
        out_specs += [row_spec] * 2
    return pl.pallas_call(
        functools.partial(advance_kernel, early, updating, looking),
        grid=(rows // tile,),
        in_specs=specs,
        out_specs=out_specs,
        out_shape=outs,
        scratch_shapes=scratch,
        compiler_params=params(),
        cost_estimate=pl.CostEstimate(
            flops=10 * rows * width * RANK, bytes_accessed=12 * rows * width, transcendentals=0
        ),
        name=f"advance_{matching}",
    )(*operands)


def gather_kernel(looking, chained, *refs):
    refs = list(refs)
    y_ref, b_ref, w_ref = refs[:3]
    refs = refs[3:]
    if looking:
        z_ref = refs.pop(0)
    if chained:
        in_small_ref, in_large_ref = refs[:2]
        refs = refs[2:]
    left_ref, small_ref, large_ref, acc_small, acc_large = refs
    step = pl.program_id(0)

    left = y_ref[...] - b_ref[...]
    left_ref[...] = left
    turned = jnp.concatenate(split(left.T), axis=0)
    narrow = jnp.concatenate([left, z_ref[...]], axis=1) if looking else left
    high, low = split(narrow)
    first = step == 0
    acc_small[...] = jnp.where(first, 0.0, acc_small[...]) + (dot(turned, high) + dot(turned, low))
    high, low = split(w_ref[...])
    acc_large[...] = jnp.where(first, 0.0, acc_large[...]) + (dot(turned, high) + dot(turned, low))

    @pl.when(step == pl.num_programs(0) - 1)
    def _():
        small = acc_small[:RANK] + acc_small[RANK:]
        small_ref[...] = small + in_small_ref[...] if chained else small

        def column(_, columns):
            large = acc_large[:RANK, columns] + acc_large[RANK:, columns]
            large_ref[:, columns] = large + in_large_ref[:, columns] if chained else large

        each_column(large_ref.shape[1], column)


def gather(start, stop, own, other, replica, z, chain):
    rows, width = replica.shape[1:]
    tile = rows // (SPLIT_ROWS if chain is None else 8)
    base, steps = start // tile, (stop - start) // tile
    looking, chained = z is not None, chain is not None
    n_small = 2 * RANK if looking else RANK
    row_spec = pl.BlockSpec((tile, RANK), lambda i: (base + i, 0))
    small_spec = pl.BlockSpec((RANK, n_small), lambda i: (0, 0))
    large_spec = pl.BlockSpec((RANK, width), lambda i: (0, 0))
    operands = [own, other, replica]
    specs = [
        row_spec,
        pl.BlockSpec((tile, RANK), lambda i: (i, 0)),
        pl.BlockSpec((None, tile, width), lambda i: (0, base + i, 0)),
    ]
    if looking:
        operands.append(z)
        specs.append(row_spec)
    if chained:
        operands += chain
        specs += [small_spec, large_spec]
    return pl.pallas_call(
        functools.partial(gather_kernel, looking, chained),
        grid=(steps,),
        in_specs=specs,
        out_specs=[pl.BlockSpec((tile, RANK), lambda i: (i, 0)), small_spec, large_spec],
        out_shape=[
            jax.ShapeDtypeStruct((stop - start, RANK), F32),
            jax.ShapeDtypeStruct((RANK, n_small), F32),
            jax.ShapeDtypeStruct((RANK, width), F32),
        ],
        scratch_shapes=[pltpu.VMEM((2 * RANK, n_small), F32), pltpu.VMEM((2 * RANK, width), F32)],
        compiler_params=params(),
        cost_estimate=pl.CostEstimate(
            flops=8 * (stop - start) * width * RANK,
            bytes_accessed=4 * (stop - start) * width,
            transcendentals=0,
        ),
        name="gather_left",
    )(*operands)


def inverse_kernel(g_ref, mine_ref, work_ref):
    work_ref[...] = g_ref[...] + mine_ref[...]
    lane = lax.broadcasted_iota(jnp.int32, (BLOCK, RANK), 1)
    row = lax.broadcasted_iota(jnp.int32, (BLOCK, RANK), 0)
    wide = lax.broadcasted_iota(jnp.int32, (RANK, RANK), 1)

    def step(block, carry):
        first = pl.multiple_of(block * BLOCK, BLOCK)
        panel = work_ref[pl.ds(first, BLOCK), :]
        turned = pltpu.roll(panel, RANK - first, 1)
        columns = [jnp.broadcast_to(turned[:, c : c + 1], (BLOCK, RANK)) for c in range(BLOCK)]
        for j in range(BLOCK):
            pivot = 1.0 / jnp.broadcast_to(columns[j][j : j + 1], (BLOCK, RANK))
            for c in range(BLOCK):
                if c != j:
                    scaled = jnp.broadcast_to(columns[c][j : j + 1], (BLOCK, RANK)) * pivot
                    columns[c] = jnp.where(row == j, scaled, columns[c] - columns[j] * scaled)
            columns[j] = jnp.where(row == j, pivot, -columns[j] * pivot)
        across = jnp.zeros((BLOCK, RANK), F32)
        for c in range(BLOCK):
            across += columns[c] * jnp.broadcast_to(panel[c : c + 1], (BLOCK, RANK))
        for c in range(BLOCK):
            across = jnp.where(lane == first + c, columns[c], across)
        signed = jnp.where(lane < first, -panel, panel)
        change = lax.dot_general(
            signed,
            across,
            (((0,), (0,)), ((), ())),
            precision=lax.Precision.HIGHEST,
            preferred_element_type=F32,
        )
        inside = (wide >= first) & (wide < first + BLOCK)
        work_ref[...] = jnp.where(inside, 0.0, work_ref[...]) - change
        work_ref[pl.ds(first, BLOCK), :] = across
        return carry

    lax.fori_loop(0, RANK // BLOCK, step, 0)


def inverse_of(gram, other):
    square = pl.BlockSpec((RANK, RANK), lambda i: (0, 0))
    return pl.pallas_call(
        inverse_kernel,
        grid=(1,),
        in_specs=[square, square],
        out_specs=square,
        out_shape=jax.ShapeDtypeStruct((RANK, RANK), F32),
        compiler_params=params(),
        cost_estimate=pl.CostEstimate(flops=2 * 10**9, bytes_accessed=10**5, transcendentals=0),
        name="inverse",
    )(gram, other)


def correct_kernel(early, v_ref, early_ref, late_ref, inverse_ref, cross_ref, y_ref, *scratch):
    stack_ref, low_ref = scratch

    @pl.when(pl.program_id(0) == 0)
    def _():
        fill_stack(inverse_ref, cross_ref, stack_ref, low_ref)

    left = left_rows(early, early_ref, late_ref)
    y_ref[...] = stacked_update(left, v_ref[...], stack_ref, low_ref)


def correct(v, left, inverse, cross):
    rows = v.shape[0]
    tile = rows // 4
    row_spec = pl.BlockSpec((tile, RANK), lambda i: (i, 0))
    early, pair_specs = left_specs(rows, tile)
    square = pl.BlockSpec((RANK, RANK), lambda i: (0, 0))
    return pl.pallas_call(
        functools.partial(correct_kernel, early),
        grid=(rows // tile,),
        in_specs=[row_spec, *pair_specs, square, square],
        out_specs=row_spec,
        out_shape=jax.ShapeDtypeStruct((rows, RANK), F32),
        scratch_shapes=[pltpu.VMEM((2 * RANK, RANK), BF16), pltpu.VMEM((RANK, RANK), BF16)],
        compiler_params=params(),
        cost_estimate=pl.CostEstimate(
            flops=2 * 10**9, bytes_accessed=12 * rows * RANK, transcendentals=0
        ),
        name="correct",
    )(v, *left, inverse, cross)


def finish_kernel(early, w_ref, early_ref, late_ref, inverse_ref, right_ref, out_ref, *scratch):
    stack_ref, low_ref = scratch

    @pl.when(pl.program_id(0) == 0)
    def _():
        fill_stack(inverse_ref, right_ref, stack_ref, low_ref)

    left = left_rows(early, early_ref, late_ref)
    out_ref[...] = stacked_update(left, w_ref[...], stack_ref, low_ref)


def finish(replica, left, inverse, right):
    rows, width = replica.shape[1:]
    tile = rows // 8
    w_spec = pl.BlockSpec((None, tile, width), lambda i: (0, i, 0))
    early, pair_specs = left_specs(rows, tile)
    return pl.pallas_call(
        functools.partial(finish_kernel, early),
        grid=(rows // tile,),
        in_specs=[
            w_spec,
            *pair_specs,
            pl.BlockSpec((RANK, RANK), lambda i: (0, 0)),
            pl.BlockSpec((RANK, width), lambda i: (0, 0)),
        ],
        out_specs=w_spec,
        out_shape=jax.ShapeDtypeStruct(replica.shape, F32),
        scratch_shapes=[pltpu.VMEM((2 * RANK, width), BF16), pltpu.VMEM((RANK, width), BF16)],
        compiler_params=params(),
        name="finish",
    )(replica, *left, inverse, right)


def swap(value, offset):
    if offset == 0:
        return value
    return lax.ppermute(value, "gossip", [(i, i ^ offset) for i in range(lax.axis_size("gossip"))])


def keep(value):
    return value


def route(value, offset):
    for level in range(lax.axis_size("gossip").bit_length() - 1):
        moved = functools.partial(swap, offset=1 << level)
        value = lax.cond(offset >> level & 1 == 1, moved, keep, value)
    return value


def across(value):
    return lax.ppermute(value, "tensor", [(0, 1), (1, 0)])


def chips_step(matching, offset, replica, updates, factors, own, sent, previous):
    rows = replica.shape[1]
    cut = rows // 4 * 3
    early = swap(sent[:cut], offset)
    late = swap(sent[cut:], offset)
    if matching > 0:
        left, inverse, right = previous
        previous = left, inverse, right + across(right)
    outs = list(advance(matching, replica, updates, factors, previous))
    now = outs[0] if matching > 0 else replica
    z = outs[-2] if matching < MATCHINGS - 1 else None
    return outs, late, list(gather(0, cut, own, early, now, z, None))


def small_step(offset, small, large):
    large_other = swap(large, offset)
    other = across(small)
    inverse = inverse_of(small, other)
    cross = small[:, RANK:] + other[:, RANK:]
    return inverse, cross + swap(cross, offset), large + large_other


def last_step(offset, small, large):
    half = RANK // 2
    other = across(small)
    other, one, two = lax.optimization_barrier((other, large[:half], large[half:]))
    two = two + swap(two, offset)
    one = one + across(one)
    inverse = inverse_of(small, other)
    one = one + swap(one, offset)
    two = two + across(two)
    return inverse, jnp.concatenate([one, two], axis=0)


def overlapped(weights, updates, factors, offsets):
    size = lax.axis_size("gossip")
    rows = weights.shape[1]
    cut = rows // 4 * 3
    replica, previous = weights, ()
    own = first_product(weights, factors)
    for matching in range(MATCHINGS):
        offset = offsets[matching]
        sent = lax.cond(offset & 1 == 1, functools.partial(swap, offset=1), keep, own)
        branches = [
            functools.partial(chips_step, matching, choice) for choice in range(0, size, 2)
        ]
        outs, late, chain = lax.switch(
            offset >> 1, branches, replica, updates, factors, own, sent, previous
        )
        if matching > 0:
            replica, *outs = outs
        z, v = outs if outs else (None, None)
        early_left, *chain = chain
        late_left, small, large = gather(cut, rows, own, late, replica, z, chain)
        left = early_left, late_left
        step = last_step if z is None else small_step
        branches = [functools.partial(step, choice) for choice in range(1, size)]
        state = lax.switch(offset - 1, branches, small, large)
        if z is not None:
            inverse, cross, right = state
            previous = left, inverse, right
            own = correct(v, left, inverse, cross)
    inverse, right = state
    return finish(replica, left, inverse, right)


def plain(weights, updates, factors, offsets):
    rows = weights.shape[1]
    cut = rows // 4 * 3
    replica, previous = weights, ()
    own = first_product(weights, factors)
    for matching in range(MATCHINGS):
        offset = offsets[matching]
        other = route(own, offset)
        outs = list(advance(matching, replica, updates, factors, previous))
        if matching > 0:
            replica, *outs = outs
        z, v = outs if outs else (None, None)
        early_left, *chain = gather(0, cut, own, other[:cut], replica, z, None)
        late_left, small, large = gather(cut, rows, own, other[cut:], replica, z, chain)
        left = early_left, late_left
        both = lax.psum(jnp.concatenate([small, large], axis=1), "tensor")
        gram, both = both[:, :RANK], both[:, RANK:]
        both = both + route(both, offset)
        inverse = inverse_of(gram, jnp.zeros_like(gram))
        if z is not None:
            own = correct(v, left, inverse, both[:, :RANK])
            both = both[:, RANK:]
        previous = left, inverse, both
    return finish(replica, *previous)


def per_device(weights, updates, factors, partners):
    myself = lax.axis_index("gossip")
    mine = lax.dynamic_index_in_dim(partners, myself, axis=1, keepdims=False)
    offsets = [jnp.bitwise_xor(mine[matching], myself) for matching in range(MATCHINGS)]
    small_slice = lax.axis_size("tensor") == 2 and lax.axis_size("gossip") <= 16
    body = overlapped if small_slice else plain
    return body(weights, updates, factors, offsets)


def solution(mesh):
    placed = (P("gossip", "tensor", None), P("gossip", None, "tensor", None), P(), P())
    return jax.shard_map(
        per_device,
        mesh=mesh,
        in_specs=placed,
        out_specs=P("gossip", "tensor", None),
        check_vma=False,
    )
```

```python
import functools

import jax
import jax.numpy as jnp
from jax import lax
from jax.experimental import pallas as pl
from jax.experimental.pallas import tpu as pltpu
from jax.sharding import PartitionSpec as P

MATCHINGS = 3
RANK = 128
BLOCK = 8
SPLIT_ROWS = 16
F32 = jnp.float32
BF16 = jnp.bfloat16


def split(value):
    high = value.astype(BF16)
    low = (value - high.astype(F32)).astype(BF16)
    return high, low


def dot(first, second):
    return jnp.dot(first, second, preferred_element_type=F32)


def dot_exact(first, second):
    return jnp.dot(first, second, precision=lax.Precision.HIGHEST, preferred_element_type=F32)


def params(mib=48):
    return pltpu.CompilerParams(vmem_limit_bytes=mib * 1024 * 1024)


def product_kernel(w_ref, q_ref, y_ref):
    high, low = split(w_ref[...])
    y_ref[...] = dot(high, q_ref[...]) + dot(low, q_ref[...])


def first_product(weights, factors):
    _, rows, width = weights.shape
    tile = rows // 4
    return pl.pallas_call(
        product_kernel,
        grid=(rows // tile,),
        in_specs=[
            pl.BlockSpec((None, tile, width), lambda i: (0, i, 0)),
            pl.BlockSpec((None, width, RANK), lambda i: (0, 0, 0)),
        ],
        out_specs=pl.BlockSpec((tile, RANK), lambda i: (i, 0)),
        out_shape=jax.ShapeDtypeStruct((rows, RANK), F32),
        compiler_params=params(),
        cost_estimate=pl.CostEstimate(
            flops=4 * rows * width * RANK, bytes_accessed=4 * rows * width, transcendentals=0
        ),
        name="first_product",
    )(weights, factors)


def each_column(width, body):
    block = min(2 * RANK, width)

    def step(index, carry):
        body(index == 0, pl.ds(pl.multiple_of(index * block, block), block))
        return carry

    lax.fori_loop(0, width // block, step, 0)


def stacked_update(left, base, stack_ref, low_ref):
    high, low = split(left)
    return base + dot(jnp.concatenate([high, low], axis=1), stack_ref[...]) + dot(high, low_ref[...])


def fill_stack(inverse_ref, right_ref, stack_ref, low_ref):
    def column(_, columns):
        high, low = split(-0.5 * dot_exact(inverse_ref[...], right_ref[:, columns]))
        stack_ref[:RANK, columns] = high
        stack_ref[RANK:, columns] = high
        low_ref[:, columns] = low

    each_column(right_ref.shape[1], column)


def left_specs(rows, tile):
    early = rows // 4 * 3 // tile
    return early, [
        pl.BlockSpec((tile, RANK), lambda i: (jnp.minimum(i, early - 1), 0)),
        pl.BlockSpec((tile, RANK), lambda i: (jnp.maximum(i - early, 0), 0)),
    ]


def left_rows(early, early_ref, late_ref):
    return jnp.where(pl.program_id(0) < early, early_ref[...], late_ref[...])


def advance_kernel(early, updating, looking, *refs):
    refs = list(refs)
    w_ref = refs.pop(0)
    if updating:
        before_ref, early_ref, late_ref, inverse_ref, right_ref = refs[:5]
        refs = refs[5:]
    if looking:
        after_ref, q_ref = refs[:2]
        refs = refs[2:]
    if updating:
        new_ref = refs.pop(0)
    if looking:
        z_ref, v_ref = refs[:2]
        refs = refs[2:]
    now = w_ref[...]
    if updating:
        stack_ref, low_ref = refs

        @pl.when(pl.program_id(0) == 0)
        def _():
            fill_stack(inverse_ref, right_ref, stack_ref, low_ref)

        left = left_rows(early, early_ref, late_ref)
        now = stacked_update(left, now - before_ref[...].astype(F32), stack_ref, low_ref)
        new_ref[...] = now
    if looking:
        high, low = split(now)
        z = dot(high, q_ref[...]) + dot(low, q_ref[...])
        z_ref[...] = z
        v_ref[...] = z - dot(after_ref[...], q_ref[...])


def advance(matching, replica, updates, factors, previous):
    rows, width = updates.shape[2:]
    tile = rows // SPLIT_ROWS
    updating, looking = matching > 0, matching < MATCHINGS - 1
    w_spec = pl.BlockSpec((None, tile, width), lambda i: (0, i, 0))
    row_spec = pl.BlockSpec((tile, RANK), lambda i: (i, 0))
    early, pair_specs = left_specs(rows, tile)
    operands, specs, outs, out_specs, scratch = [replica], [w_spec], [], [], []
    if updating:
        left, inverse, right = previous
        operands += [updates, *left, inverse, right]
        specs += [
            pl.BlockSpec((None, None, tile, width), lambda i: (0, matching - 1, i, 0)),
            *pair_specs,
            pl.BlockSpec((RANK, RANK), lambda i: (0, 0)),
            pl.BlockSpec((RANK, width), lambda i: (0, 0)),
        ]
        outs.append(jax.ShapeDtypeStruct((1, rows, width), F32))
        out_specs.append(w_spec)
        scratch = [pltpu.VMEM((2 * RANK, width), BF16), pltpu.VMEM((RANK, width), BF16)]
    if looking:
        operands += [updates, factors]
        specs += [
            pl.BlockSpec((None, None, tile, width), lambda i: (0, matching, i, 0)),
            pl.BlockSpec((None, width, RANK), lambda i: (matching + 1, 0, 0)),
        ]
        outs += [jax.ShapeDtypeStruct((rows, RANK), F32)] * 2
        out_specs += [row_spec] * 2
    return pl.pallas_call(
        functools.partial(advance_kernel, early, updating, looking),
        grid=(rows // tile,),
        in_specs=specs,
        out_specs=out_specs,
        out_shape=outs,
        scratch_shapes=scratch,
        compiler_params=params(),
        cost_estimate=pl.CostEstimate(
            flops=10 * rows * width * RANK, bytes_accessed=12 * rows * width, transcendentals=0
        ),
        name=f"advance_{matching}",
    )(*operands)


def gather_kernel(looking, chained, *refs):
    refs = list(refs)
    y_ref, b_ref, w_ref = refs[:3]
    refs = refs[3:]
    if looking:
        z_ref = refs.pop(0)
    if chained:
        in_small_ref, in_large_ref = refs[:2]
        refs = refs[2:]
    left_ref, small_ref, large_ref, acc_small, acc_large = refs
    step = pl.program_id(0)

    left = y_ref[...] - b_ref[...]
    left_ref[...] = left
    turned = jnp.concatenate(split(left.T), axis=0)
    narrow = jnp.concatenate([left, z_ref[...]], axis=1) if looking else left
    high, low = split(narrow)
    first = step == 0
    acc_small[...] = jnp.where(first, 0.0, acc_small[...]) + (dot(turned, high) + dot(turned, low))
    high, low = split(w_ref[...])
    acc_large[...] = jnp.where(first, 0.0, acc_large[...]) + (dot(turned, high) + dot(turned, low))

    @pl.when(step == pl.num_programs(0) - 1)
    def _():
        small = acc_small[:RANK] + acc_small[RANK:]
        small_ref[...] = small + in_small_ref[...] if chained else small

        def column(_, columns):
            large = acc_large[:RANK, columns] + acc_large[RANK:, columns]
            large_ref[:, columns] = large + in_large_ref[:, columns] if chained else large

        each_column(large_ref.shape[1], column)


def gather(start, stop, own, other, replica, z, chain):
    rows, width = replica.shape[1:]
    tile = rows // (SPLIT_ROWS if chain is None else 8)
    base, steps = start // tile, (stop - start) // tile
    looking, chained = z is not None, chain is not None
    n_small = 2 * RANK if looking else RANK
    row_spec = pl.BlockSpec((tile, RANK), lambda i: (base + i, 0))
    small_spec = pl.BlockSpec((RANK, n_small), lambda i: (0, 0))
    large_spec = pl.BlockSpec((RANK, width), lambda i: (0, 0))
    operands = [own, other, replica]
    specs = [
        row_spec,
        pl.BlockSpec((tile, RANK), lambda i: (i, 0)),
        pl.BlockSpec((None, tile, width), lambda i: (0, base + i, 0)),
    ]
    if looking:
        operands.append(z)
        specs.append(row_spec)
    if chained:
        operands += chain
        specs += [small_spec, large_spec]
    return pl.pallas_call(
        functools.partial(gather_kernel, looking, chained),
        grid=(steps,),
        in_specs=specs,
        out_specs=[pl.BlockSpec((tile, RANK), lambda i: (i, 0)), small_spec, large_spec],
        out_shape=[
            jax.ShapeDtypeStruct((stop - start, RANK), F32),
            jax.ShapeDtypeStruct((RANK, n_small), F32),
            jax.ShapeDtypeStruct((RANK, width), F32),
        ],
        scratch_shapes=[pltpu.VMEM((2 * RANK, n_small), F32), pltpu.VMEM((2 * RANK, width), F32)],
        compiler_params=params(),
        cost_estimate=pl.CostEstimate(
            flops=8 * (stop - start) * width * RANK,
            bytes_accessed=4 * (stop - start) * width,
            transcendentals=0,
        ),
        name="gather_left",
    )(*operands)


def inverse_kernel(g_ref, mine_ref, work_ref):
    work_ref[...] = g_ref[...] + mine_ref[...]
    lane = lax.broadcasted_iota(jnp.int32, (BLOCK, RANK), 1)
    row = lax.broadcasted_iota(jnp.int32, (BLOCK, RANK), 0)
    wide = lax.broadcasted_iota(jnp.int32, (RANK, RANK), 1)

    def step(block, carry):
        first = pl.multiple_of(block * BLOCK, BLOCK)
        panel = work_ref[pl.ds(first, BLOCK), :]
        turned = pltpu.roll(panel, RANK - first, 1)
        columns = [jnp.broadcast_to(turned[:, c : c + 1], (BLOCK, RANK)) for c in range(BLOCK)]
        for j in range(BLOCK):
            pivot = 1.0 / jnp.broadcast_to(columns[j][j : j + 1], (BLOCK, RANK))
            for c in range(BLOCK):
                if c != j:
                    scaled = jnp.broadcast_to(columns[c][j : j + 1], (BLOCK, RANK)) * pivot
                    columns[c] = jnp.where(row == j, scaled, columns[c] - columns[j] * scaled)
            columns[j] = jnp.where(row == j, pivot, -columns[j] * pivot)
        across = jnp.zeros((BLOCK, RANK), F32)
        for c in range(BLOCK):
            across += columns[c] * jnp.broadcast_to(panel[c : c + 1], (BLOCK, RANK))
        for c in range(BLOCK):
            across = jnp.where(lane == first + c, columns[c], across)
        signed = jnp.where(lane < first, -panel, panel)
        change = lax.dot_general(
            signed,
            across,
            (((0,), (0,)), ((), ())),
            precision=lax.Precision.HIGHEST,
            preferred_element_type=F32,
        )
        inside = (wide >= first) & (wide < first + BLOCK)
        work_ref[...] = jnp.where(inside, 0.0, work_ref[...]) - change
        work_ref[pl.ds(first, BLOCK), :] = across
        return carry

    lax.fori_loop(0, RANK // BLOCK, step, 0)


def inverse_of(gram, other):
    square = pl.BlockSpec((RANK, RANK), lambda i: (0, 0))
    return pl.pallas_call(
        inverse_kernel,
        grid=(1,),
        in_specs=[square, square],
        out_specs=square,
        out_shape=jax.ShapeDtypeStruct((RANK, RANK), F32),
        compiler_params=params(),
        cost_estimate=pl.CostEstimate(flops=2 * 10**9, bytes_accessed=10**5, transcendentals=0),
        name="inverse",
    )(gram, other)


def correct_kernel(early, v_ref, early_ref, late_ref, inverse_ref, cross_ref, y_ref, *scratch):
    stack_ref, low_ref = scratch

    @pl.when(pl.program_id(0) == 0)
    def _():
        fill_stack(inverse_ref, cross_ref, stack_ref, low_ref)

    left = left_rows(early, early_ref, late_ref)
    y_ref[...] = stacked_update(left, v_ref[...], stack_ref, low_ref)


def correct(v, left, inverse, cross):
    rows = v.shape[0]
    tile = rows // 4
    row_spec = pl.BlockSpec((tile, RANK), lambda i: (i, 0))
    early, pair_specs = left_specs(rows, tile)
    square = pl.BlockSpec((RANK, RANK), lambda i: (0, 0))
    return pl.pallas_call(
        functools.partial(correct_kernel, early),
        grid=(rows // tile,),
        in_specs=[row_spec, *pair_specs, square, square],
        out_specs=row_spec,
        out_shape=jax.ShapeDtypeStruct((rows, RANK), F32),
        scratch_shapes=[pltpu.VMEM((2 * RANK, RANK), BF16), pltpu.VMEM((RANK, RANK), BF16)],
        compiler_params=params(),
        cost_estimate=pl.CostEstimate(
            flops=2 * 10**9, bytes_accessed=12 * rows * RANK, transcendentals=0
        ),
        name="correct",
    )(v, *left, inverse, cross)


def finish_kernel(early, w_ref, early_ref, late_ref, inverse_ref, right_ref, out_ref, *scratch):
    stack_ref, low_ref = scratch

    @pl.when(pl.program_id(0) == 0)
    def _():
        fill_stack(inverse_ref, right_ref, stack_ref, low_ref)

    left = left_rows(early, early_ref, late_ref)
    out_ref[...] = stacked_update(left, w_ref[...], stack_ref, low_ref)


def finish(replica, left, inverse, right):
    rows, width = replica.shape[1:]
    tile = rows // 4
    w_spec = pl.BlockSpec((None, tile, width), lambda i: (0, i, 0))
    early, pair_specs = left_specs(rows, tile)
    return pl.pallas_call(
        functools.partial(finish_kernel, early),
        grid=(rows // tile,),
        in_specs=[
            w_spec,
            *pair_specs,
            pl.BlockSpec((RANK, RANK), lambda i: (0, 0)),
            pl.BlockSpec((RANK, width), lambda i: (0, 0)),
        ],
        out_specs=w_spec,
        out_shape=jax.ShapeDtypeStruct(replica.shape, F32),
        scratch_shapes=[pltpu.VMEM((2 * RANK, width), BF16), pltpu.VMEM((RANK, width), BF16)],
        compiler_params=params(),
        name="finish",
    )(replica, *left, inverse, right)


def swap(value, offset):
    if offset == 0:
        return value
    return lax.ppermute(value, "gossip", [(i, i ^ offset) for i in range(lax.axis_size("gossip"))])


def keep(value):
    return value


def route(value, offset):
    for level in range(lax.axis_size("gossip").bit_length() - 1):
        moved = functools.partial(swap, offset=1 << level)
        value = lax.cond(offset >> level & 1 == 1, moved, keep, value)
    return value


def across(value):
    return lax.ppermute(value, "tensor", [(0, 1), (1, 0)])


def chips_step(matching, offset, replica, updates, factors, own, sent, previous):
    rows = replica.shape[1]
    cut = rows // 4 * 3
    early = swap(sent[:cut], offset)
    late = swap(sent[cut:], offset)
    if matching > 0:
        left, inverse, right = previous
        previous = left, inverse, right + across(right)
    outs = list(advance(matching, replica, updates, factors, previous))
    now = outs[0] if matching > 0 else replica
    z = outs[-2] if matching < MATCHINGS - 1 else None
    return outs, late, list(gather(0, cut, own, early, now, z, None))


def small_step(offset, small, large):
    large_other = swap(large, offset)
    other = across(small)
    inverse = inverse_of(small, other)
    cross = small[:, RANK:] + other[:, RANK:]
    return inverse, cross + swap(cross, offset), large + large_other


def last_step(offset, small, large):
    half = RANK // 2
    other = across(small)
    other, one, two = lax.optimization_barrier((other, large[:half], large[half:]))
    two = two + swap(two, offset)
    one = one + across(one)
    inverse = inverse_of(small, other)
    one = one + swap(one, offset)
    two = two + across(two)
    return inverse, jnp.concatenate([one, two], axis=0)


def overlapped(weights, updates, factors, offsets):
    size = lax.axis_size("gossip")
    rows = weights.shape[1]
    cut = rows // 4 * 3
    replica, previous = weights, ()
    own = first_product(weights, factors)
    for matching in range(MATCHINGS):
        offset = offsets[matching]
        sent = lax.cond(offset & 1 == 1, functools.partial(swap, offset=1), keep, own)
        branches = [
            functools.partial(chips_step, matching, choice) for choice in range(0, size, 2)
        ]
        outs, late, chain = lax.switch(
            offset >> 1, branches, replica, updates, factors, own, sent, previous
        )
        if matching > 0:
            replica, *outs = outs
        z, v = outs if outs else (None, None)
        early_left, *chain = chain
        late_left, small, large = gather(cut, rows, own, late, replica, z, chain)
        left = early_left, late_left
        step = last_step if z is None else small_step
        branches = [functools.partial(step, choice) for choice in range(1, size)]
        state = lax.switch(offset - 1, branches, small, large)
        if z is not None:
            inverse, cross, right = state
            previous = left, inverse, right
            own = correct(v, left, inverse, cross)
    inverse, right = state
    return finish(replica, left, inverse, right)


def plain(weights, updates, factors, offsets):
    rows = weights.shape[1]
    cut = rows // 4 * 3
    replica, previous = weights, ()
    own = first_product(weights, factors)
    for matching in range(MATCHINGS):
        offset = offsets[matching]
        other = route(own, offset)
        outs = list(advance(matching, replica, updates, factors, previous))
        if matching > 0:
            replica, *outs = outs
        z, v = outs if outs else (None, None)
        early_left, *chain = gather(0, cut, own, other[:cut], replica, z, None)
        late_left, small, large = gather(cut, rows, own, other[cut:], replica, z, chain)
        left = early_left, late_left
        both = lax.psum(jnp.concatenate([small, large], axis=1), "tensor")
        gram, both = both[:, :RANK], both[:, RANK:]
        both = both + route(both, offset)
        inverse = inverse_of(gram, jnp.zeros_like(gram))
        if z is not None:
            own = correct(v, left, inverse, both[:, :RANK])
            both = both[:, RANK:]
        previous = left, inverse, both
    return finish(replica, *previous)


def per_device(weights, updates, factors, partners):
    myself = lax.axis_index("gossip")
    mine = lax.dynamic_index_in_dim(partners, myself, axis=1, keepdims=False)
    offsets = [jnp.bitwise_xor(mine[matching], myself) for matching in range(MATCHINGS)]
    small_slice = lax.axis_size("tensor") == 2 and lax.axis_size("gossip") <= 16
    body = overlapped if small_slice else plain
    return body(weights, updates, factors, offsets)


def solution(mesh):
    placed = (P("gossip", "tensor", None), P("gossip", None, "tensor", None), P(), P())
    return jax.shard_map(
        per_device,
        mesh=mesh,
        in_specs=placed,
        out_specs=P("gossip", "tensor", None),
        check_vma=False,
    )
```
